32 devices in a mesh: round: 4 (over z), stab: 8 (over y, x, core).
Axes of the slice: x: 2, y: 2, z: 4, core: 2. Of those that a mesh axis runs over, the one named last changes fastest.
Arguments:
- inputs: bfloat16 [32, 896, 512], P('round', 'stab'), may hold values from -6 to 6
- labels: int32 [32, 896], P('round', 'stab'), may hold values 0 or 1
- neighbours: int32 [224, 16], replicated, may hold values from 0 to 209, as said below
- space_in_weights: bfloat16 [512, 1536], replicated
- space_out_weights: bfloat16 [512, 512], replicated, may hold values from -0.25 to 0.25
- space_gain: float32 [512], replicated, may hold values from 0.5 to 1.5
- time_in_weights: bfloat16 [512, 1536], replicated
- time_out_weights: bfloat16 [512, 512], replicated, may hold values from -0.25 to 0.25
- time_gain: float32 [512], replicated, may hold values from 0.5 to 1.5
- readout: float32 [512], replicated, may hold values from -1 to 1
Outputs:
- grad_inputs: float32 [32, 896, 512], P('round', 'stab')
The draws below stay inside these ranges and needn't reach their ends.
Inputs may be any that keep to these rules, and one draw needn't show every extreme that they name: `neighbours`: row b lists 16 distinct blocks below 210; each such block b lists itself.
All inputs are finite; a program needn't handle non-finite values. No bound on the sum of `labels` on one device may be relied on, other than what follows from the above.
Results may differ from the reference program's by a relative error of at most 0.0085.
Values may be sent and summed in bfloat16 or wider, within the bound.
A program may use at most 320 MiB of HBM per device.

```python
import jax
import jax.numpy as jnp
from jax import lax

D = 512
HEADS = 8
HEAD_DIM = 64
STABS = 896
STABS_REAL = 840
BLOCK = 4
LINKS = 16
ROUNDS = 32


def draw_neighbours(key, part):
    real_blocks = STABS_REAL // BLOCK
    all_blocks = STABS // BLOCK
    scores = jax.random.randint(key, (all_blocks, real_blocks), 0, 1 << 20) * 256 + jnp.arange(real_blocks)[None, :]
    itself = jnp.arange(all_blocks)[:, None] == jnp.arange(real_blocks)[None, :]
    scores = scores + jnp.where(itself, 1 << 28, 0)
    return lax.top_k(scores, LINKS)[1].astype(jnp.int32)


def input_weights(key):
    base = jax.random.normal(key, (D, 3, D), jnp.float32) * D ** (-0.5)
    return base.reshape(D, 3 * D)


def draw_space_in_weights(key, part):
    return input_weights(jax.random.fold_in(key, 11)).astype(jnp.bfloat16)


def draw_time_in_weights(key, part):
    return input_weights(jax.random.fold_in(key, 12)).astype(jnp.bfloat16)


def place_ends(entries, key, least, largest):
    dims = entries.shape
    place = [jax.random.randint(jax.random.fold_in(key, axis), (), 0, dims[axis]) for axis in range(len(dims))]
    entries = entries.at[tuple(place)].set(least)
    longest = dims.index(max(dims))
    place[longest] = (place[longest] + 1) % dims[longest]
    return entries.at[tuple(place)].set(largest)


def steps_of(stream_key, shape, cuts, low, largest):
    def one(axis_at, blocks):
        draws = jax.random.uniform(jax.random.fold_in(jax.random.fold_in(stream_key, 6), axis_at), (blocks,), jnp.float32, low / len(cuts), largest / len(cuts))
        return jnp.repeat(jnp.exp(draws), shape[axis_at] // blocks).reshape((-1,) + (1,) * (len(shape) - axis_at - 1))

    level = one(*cuts[0])
    for cut in cuts[1:]:
        level = level * one(*cut)
    return level


def bell_draw(key, extent, scale, most, cuts=(), kind=jnp.bfloat16):
    result = jax.random.normal(key, extent, jnp.float32) * scale
    if len(cuts) > 0:
        result = steps_of(key, extent, cuts, -0.22, 0.18) * result
    return jnp.clip(result, min=-most, max=most).astype(kind)


def setup_inputs(seed: int = 0) -> dict:
    key_list = jax.random.split(jax.random.key(seed), 11)
    inputs = bell_draw(key_list[0], (ROUNDS, STABS, D), 1.0, 6.0, ((0, 4), (1, 8)))
    labels = place_ends((jax.random.randint(key_list[1], (ROUNDS, STABS), 0, 2) < 1).astype(jnp.int32), jax.random.fold_in(key_list[1], 1), 0, 1)
    neighbours = draw_neighbours(jax.random.fold_in(key_list[10], 71), 0)
    space_in_weights = draw_space_in_weights(jax.random.fold_in(key_list[10], 71), 0)
    space_out_weights = bell_draw(key_list[4], (D, D), D ** -0.5, 0.25)
    space_gain = jnp.clip(1.0 + 0.1 * jax.random.normal(key_list[5], (D,), jnp.float32), 0.5, 1.5)
    time_in_weights = draw_time_in_weights(jax.random.fold_in(key_list[10], 71), 0)
    time_out_weights = bell_draw(key_list[7], (D, D), D ** -0.5, 0.25)
    time_gain = jnp.clip(1.0 + 0.1 * jax.random.normal(key_list[8], (D,), jnp.float32), 0.5, 1.5)
    readout = bell_draw(key_list[9], (D,), 0.18, 1.0, (), jnp.float32)
    return dict(inputs=inputs, labels=labels, neighbours=neighbours, space_in_weights=space_in_weights, space_out_weights=space_out_weights, space_gain=space_gain, time_in_weights=time_in_weights, time_out_weights=time_out_weights, time_gain=time_gain, readout=readout)


EPSILON = 1e-06
MASKED_SCORE = -1e+30

def contract(form, first_operand, second_operand):
    return jnp.einsum(form, first_operand.astype(jnp.float32), second_operand.astype(jnp.float32))

def norm_rows(hidden, gain):
    inverse = lax.rsqrt(lax.optimization_barrier(jnp.mean(hidden * hidden, axis=-1, keepdims=True)) + EPSILON)
    return ((hidden * inverse * gain).astype(jnp.bfloat16), inverse)

def norm_back(hidden, inverse, gain, upstream):
    scaled = upstream * gain
    inner = lax.optimization_barrier(jnp.mean(hidden * scaled, axis=-1, keepdims=True))
    return inverse * scaled - hidden * inverse * inverse * inverse * inner

def block_keys(field, neighbours):
    head_depth = field.shape[0]
    blocked = field.reshape(head_depth, -1, BLOCK)
    return blocked[:, neighbours].reshape(head_depth, neighbours.shape[0], -1)

def spread_back(near_grad, neighbours):
    head_depth = near_grad.shape[0]
    block_count = neighbours.shape[0]
    pieces = near_grad.reshape(head_depth, block_count, neighbours.shape[1], BLOCK)
    summed = jnp.zeros((head_depth, block_count, BLOCK), near_grad.dtype).at[:, neighbours].add(pieces)
    return summed.reshape(head_depth, -1)

def space_scores(queries, key_rows, neighbours):
    head_depth = queries.shape[0]
    factor = head_depth ** (-0.5)
    query_blocks = queries.reshape(head_depth, -1, BLOCK)
    near_keys = block_keys(key_rows, neighbours)
    return (contract('dni,dnj->nij', query_blocks, near_keys) * factor, query_blocks, near_keys, factor)

def space_forward(queries, key_rows, values, neighbours):
    scores, query_blocks, near_keys, factor = space_scores(queries, key_rows, neighbours)
    highest = lax.optimization_barrier(jnp.max(scores, axis=-1, keepdims=True))
    logsum = highest + jnp.log(lax.optimization_barrier(jnp.sum(jnp.exp(scores - highest), axis=-1, keepdims=True)))
    weights = jnp.exp(scores - logsum).astype(jnp.bfloat16)
    attended = contract('nij,dnj->dni', weights, block_keys(values, neighbours)).astype(jnp.bfloat16)
    return (attended.reshape(queries.shape), logsum)

def space_backward(queries, key_rows, values, neighbours, attended, grad_rows, logsum):
    scores, query_blocks, near_keys, factor = space_scores(queries, key_rows, neighbours)
    near_values = block_keys(values, neighbours)
    probability = jnp.exp(scores - logsum)
    weights = probability.astype(jnp.bfloat16)
    grad_blocks = grad_rows.reshape(query_blocks.shape)
    spread = lax.optimization_barrier(jnp.sum(grad_rows.astype(jnp.float32) * attended.astype(jnp.float32), axis=0)).reshape(-1, BLOCK)[:, :, None]
    grad_near_values = contract('nij,dni->dnj', weights, grad_blocks)
    grad_weights = contract('dni,dnj->nij', grad_blocks, near_values)
    grad_scores = (probability * (grad_weights - spread) * factor).astype(jnp.bfloat16)
    grad_queries = contract('nij,dnj->dni', grad_scores, near_keys).reshape(queries.shape)
    grad_near_keys = contract('nij,dni->dnj', grad_scores, query_blocks)
    return (grad_queries, spread_back(grad_near_keys, neighbours), spread_back(grad_near_values, neighbours))

def causal_scores(queries, key_rows, query_offset, key_offset):
    query_len, pair_count, span = queries.shape
    key_len = key_rows.shape[0]
    query_heads = queries.reshape(query_len, pair_count, 2, span // 2)
    key_heads = key_rows.reshape(key_len, pair_count, 2, span // 2)
    factor = (span // 2) ** (-0.5)
    scores = contract('qphd,kphd->phqk', query_heads, key_heads) * factor
    allowed = (query_offset + jnp.arange(query_len))[:, None] >= (key_offset + jnp.arange(key_len))[None, :]
    return (jnp.where(allowed, scores, MASKED_SCORE), query_heads, key_heads, factor)

def time_forward(queries, key_rows, values, query_offset, key_offset):
    scores, query_heads, key_heads, factor = causal_scores(queries, key_rows, query_offset, key_offset)
    value_heads = values.reshape(key_heads.shape)
    highest = lax.optimization_barrier(jnp.max(scores, axis=-1, keepdims=True))
    logsum = highest + jnp.log(lax.optimization_barrier(jnp.sum(jnp.exp(scores - highest), axis=-1, keepdims=True)))
    weights = jnp.exp(scores - logsum).astype(jnp.bfloat16)
    attended = contract('phqk,kphd->qphd', weights, value_heads).astype(jnp.bfloat16)
    return (attended.reshape(queries.shape), jnp.transpose(logsum[..., 0], (2, 0, 1)))

def delta_rows(attended, grad_rows):
    product = attended.astype(jnp.float32) * grad_rows.astype(jnp.float32)
    return lax.optimization_barrier(jnp.sum(product.reshape(attended.shape[0], attended.shape[1], 2, -1), axis=-1))

def time_backward(queries, key_rows, values, grad_rows, logsum, spread, query_offset, key_offset):
    scores, query_heads, key_heads, factor = causal_scores(queries, key_rows, query_offset, key_offset)
    value_heads = values.reshape(key_heads.shape)
    grad_heads = grad_rows.reshape(query_heads.shape)
    probability = jnp.exp(scores - jnp.transpose(logsum, (1, 2, 0))[..., None])
    weights = probability.astype(jnp.bfloat16)
    grad_values = contract('phqk,qphd->kphd', weights, grad_heads)
    grad_weights = contract('qphd,kphd->phqk', grad_heads, value_heads)
    grad_scores = (probability * (grad_weights - jnp.transpose(spread, (1, 2, 0))[..., None]) * factor).astype(jnp.bfloat16)
    grad_queries = contract('phqk,kphd->qphd', grad_scores, key_heads)
    grad_keys = contract('phqk,qphd->kphd', grad_scores, query_heads)
    return (grad_queries.reshape(queries.shape), grad_keys.reshape(key_rows.shape), grad_values.reshape(key_rows.shape))

def readout_grad(after_time, readout, targets, real_mask):
    logits = lax.optimization_barrier(jnp.sum(after_time * readout, axis=-1))
    grad_logits = (jax.nn.sigmoid(logits) - targets.astype(jnp.float32)) * real_mask
    return grad_logits[..., None] * readout

def reference(inputs, labels, neighbours, space_in_weights, space_out_weights, space_gain, time_in_weights, time_out_weights, time_gain, readout):
    rounds, stab_count, features = inputs.shape
    space_four = space_in_weights.reshape(features, 3, HEADS, HEAD_DIM)
    space_three = space_out_weights.reshape(HEADS, HEAD_DIM, features)
    time_three = time_in_weights.reshape(features, 3, features)
    attend = jax.vmap(space_forward, in_axes=(0, 0, 0, None))
    revert = jax.vmap(space_backward, in_axes=(0, 0, 0, None, 0, 0, 0))

    def space_prepare(round_rows):
        widened = round_rows.astype(jnp.float32)
        normed, inverse = norm_rows(widened, space_gain)
        triple = contract('sd,dchk->chks', normed, space_four).astype(jnp.bfloat16)
        attended, logsum = attend(triple[0], triple[1], triple[2], neighbours)
        return (widened, inverse, triple, attended, logsum)

    def space_ahead(round_rows):
        widened, inverse, triple, attended, logsum = space_prepare(round_rows)
        return widened + contract('hks,hkd->sd', attended, space_three)
    after_space = lax.map(space_ahead, inputs)
    blocks = stab_count // BLOCK
    block_rows = jnp.transpose(after_space.reshape(rounds, blocks, BLOCK, features), (1, 0, 2, 3))
    block_labels = jnp.transpose(labels.reshape(rounds, blocks, BLOCK), (1, 0, 2))
    block_real = (jnp.arange(stab_count) < STABS_REAL).astype(jnp.float32).reshape(blocks, BLOCK)

    def time_block(packed):
        row_block, targets, real_mask = packed
        normed, inverse = norm_rows(row_block, time_gain)
        triple = contract('rsd,dce->crse', normed, time_three).astype(jnp.bfloat16)
        triple = triple.reshape(3, rounds, BLOCK * HEADS // 2, 2 * HEAD_DIM)
        attended, logsum = time_forward(triple[0], triple[1], triple[2], 0, 0)
        after_time = row_block + jnp.dot(attended.reshape(-1, features), time_out_weights, preferred_element_type=jnp.float32).reshape(row_block.shape)
        grad_after = readout_grad(after_time, readout, targets, real_mask)
        grad_attended = contract('td,ed->te', grad_after.astype(jnp.bfloat16).reshape(-1, features), time_out_weights).astype(jnp.bfloat16).reshape(attended.shape)
        spread = delta_rows(attended, grad_attended)
        grad_three = time_backward(triple[0], triple[1], triple[2], grad_attended, logsum, spread, 0, 0)
        stacked = jnp.stack(grad_three).astype(jnp.bfloat16).reshape(3, rounds, BLOCK, features)
        grad_normed = contract('crse,dce->rsd', stacked, time_three)
        return grad_after + norm_back(row_block, inverse, time_gain, grad_normed)
    grad_blocks = lax.map(time_block, (block_rows, block_labels, block_real))
    grad_space_rows = jnp.transpose(grad_blocks, (1, 0, 2, 3)).reshape(rounds, stab_count, features)

    def space_behind(packed):
        round_rows, upstream = packed
        widened, inverse, triple, attended, logsum = space_prepare(round_rows)
        grad_attended = contract('sd,hkd->hks', upstream.astype(jnp.bfloat16), space_three).astype(jnp.bfloat16)
        grad_three = revert(triple[0], triple[1], triple[2], neighbours, attended, grad_attended, logsum)
        stacked = jnp.stack(grad_three).astype(jnp.bfloat16)
        grad_normed = contract('chks,dchk->sd', stacked, space_four)
        return upstream + norm_back(widened, inverse, space_gain, grad_normed)
    return lax.map(space_behind, (inputs, grad_space_rows))
```

```python
import functools

import jax
import jax.numpy as jnp
from jax import lax
from jax.experimental import pallas as pl
from jax.experimental.pallas import tpu as pltpu
from jax.sharding import PartitionSpec as P

HEADS = 8
HEAD_DIM = 64
STABS_REAL = 840
BLOCK = 4
PAIR = 2 * HEAD_DIM
CHUNK = 128
GROUP = 128

EPSILON = 1e-06
MASKED_SCORE = -1e30
FACTOR = HEAD_DIM ** (-0.5)
VMEM_LIMIT = 50 * 1024 * 1024


def dot(first, second):
    return jnp.dot(first, second, preferred_element_type=jnp.float32)


def dot_nt(first, second):
    return lax.dot_general(
        first, second, (((1,), (1,)), ((), ())), preferred_element_type=jnp.float32
    )


def dot_tn(first, second):
    return lax.dot_general(
        first, second, (((0,), (0,)), ((), ())), preferred_element_type=jnp.float32
    )


def inverse_rms(hidden):
    return lax.rsqrt(jnp.mean(hidden * hidden, axis=-1, keepdims=True) + EPSILON)


def norm_back(hidden, inverse, gain, upstream):
    scaled = upstream * gain
    inner = jnp.mean(hidden * scaled, axis=-1, keepdims=True)
    return inverse * scaled - hidden * (inverse * inverse * inverse * inner)


def softmax_rows(scores):
    highest = jnp.max(scores, axis=-1, keepdims=True)
    weights = jnp.exp(scores - highest)
    total = jnp.sum(weights, axis=-1, keepdims=True)
    return (weights * (1.0 / total)).astype(jnp.bfloat16)


def space_forward_kernel(
    x_ref, near_ref, gain_ref, wq_ref, wk_ref, wv_ref, wo_ref,
    h_ref, q_ref, k_ref, v_ref, o_ref, p_ref,
    n_scr, bias_scr, acc_scr,
):
    step = pl.program_id(0)
    stabs = x_ref.shape[0]
    blocks, links = near_ref.shape

    @pl.when(step == 0)
    def _():
        x = x_ref[...].astype(jnp.float32)
        n_scr[...] = (x * inverse_rms(x) * gain_ref[...]).astype(jnp.bfloat16)
        acc_scr[...] = x
        lanes = lax.broadcasted_iota(jnp.int32, (blocks, blocks), 1)
        near = near_ref[...]
        listed = jnp.zeros((blocks, blocks), jnp.float32)
        for link in range(links):
            listed = jnp.where(lanes == near[:, link : link + 1], 1.0, listed)
        owner = lax.broadcasted_iota(jnp.int32, (stabs, blocks), 0) // BLOCK
        column = lax.broadcasted_iota(jnp.int32, (stabs, blocks), 1)
        widen = jnp.where(owner == column, 1.0, 0.0).astype(jnp.bfloat16)
        rows = dot(widen, listed.astype(jnp.bfloat16)).astype(jnp.bfloat16)
        bias_scr[...] = jnp.where(dot_nt(rows, widen) > 0.5, 0.0, MASKED_SCORE)

    n = n_scr[...]
    q_ref[...] = dot(n, wq_ref[...]).astype(jnp.bfloat16)
    k_ref[...] = dot(n, wk_ref[...]).astype(jnp.bfloat16)
    v_ref[...] = dot(n, wv_ref[...]).astype(jnp.bfloat16)
    for head in range(2):
        cols = slice(head * HEAD_DIM, (head + 1) * HEAD_DIM)
        keys = k_ref[:, cols]
        values = v_ref[:, cols]
        for start in range(0, stabs, CHUNK):
            rows = slice(start, start + CHUNK)
            scores = dot_nt(q_ref[rows, cols] * FACTOR, keys) + bias_scr[rows, :]
            weights = softmax_rows(scores)
            p_ref[head, rows, :] = weights
            o_ref[rows, cols] = dot(weights, values).astype(jnp.bfloat16)
    acc_scr[...] += dot(o_ref[...], wo_ref[...])

    @pl.when(step == pl.num_programs(0) - 1)
    def _():
        h_ref[...] = acc_scr[...].astype(jnp.bfloat16)


def space_backward_kernel(
    x_ref, gain_ref, g_ref, q_ref, k_ref, v_ref, o_ref, p_ref,
    wq_ref, wk_ref, wv_ref, wo_ref,
    out_ref,
    gn_scr, go_scr, gs_scr, dq_scr, dk_scr, dv_scr,
):
    step = pl.program_id(0)
    stabs = x_ref.shape[0]
    go = dot_nt(g_ref[...], wo_ref[...]).astype(jnp.bfloat16)
    go_scr[...] = go
    product = go.astype(jnp.float32) * o_ref[...].astype(jnp.float32)
    q_turned = q_ref[...].T
    go_turned = go.T
    for head in range(2):
        cols = slice(head * HEAD_DIM, (head + 1) * HEAD_DIM)
        keys = k_ref[:, cols]
        values = v_ref[:, cols]
        delta = jnp.sum(product[:, cols], axis=-1, keepdims=True)
        for start in range(0, stabs, CHUNK):
            rows = slice(start, start + CHUNK)
            grad_weights = dot_nt(go_scr[rows, cols], values)
            weights = p_ref[head, rows, :].astype(jnp.float32)
            grad_scores = (
                weights * ((grad_weights - delta[start : start + CHUNK]) * FACTOR)
            ).astype(jnp.bfloat16)
            gs_scr[rows, :] = grad_scores
            dq_scr[rows, cols] = dot(grad_scores, keys).astype(jnp.bfloat16)
        dk_scr[cols, :] = dot(q_turned[cols, :], gs_scr[...]).astype(jnp.bfloat16)
        dv_scr[cols, :] = dot(go_turned[cols, :], p_ref[head]).astype(jnp.bfloat16)
    part = (
        dot_nt(dq_scr[...], wq_ref[...])
        + dot_nt(dk_scr[...].T, wk_ref[...])
        + dot_nt(dv_scr[...].T, wv_ref[...])
    )

    @pl.when(step == 0)
    def _():
        gn_scr[...] = part

    @pl.when(step > 0)
    def _():
        gn_scr[...] += part

    @pl.when(step == pl.num_programs(0) - 1)
    def _():
        x = x_ref[...].astype(jnp.float32)
        back = norm_back(x, inverse_rms(x), gain_ref[...], gn_scr[...])
        out_ref[...] = (g_ref[...].astype(jnp.float32) + back).astype(jnp.bfloat16)


def time_kernel(
    width, h_ref, side_ref, gain_ref, readout_ref, win_ref, wout_ref,
    g_ref,
    qkv_scr, p_scr, o_scr, d_scr,
):
    tokens, features = h_ref.shape
    hidden = h_ref[...].astype(jnp.float32)
    inverse = inverse_rms(hidden)
    gain = gain_ref[...]
    normed = (hidden * inverse * gain).astype(jnp.bfloat16)
    qkv_scr[...] = dot(normed, win_ref[...]).astype(jnp.bfloat16)
    left = lax.broadcasted_iota(jnp.int32, (tokens, tokens), 0)
    right = lax.broadcasted_iota(jnp.int32, (tokens, tokens), 1)
    kept = ((left % width) == (right % width)) & (right <= left)
    bias = jnp.where(kept, 0.0, MASKED_SCORE)

    def part(index, head):
        start = index * features + head * HEAD_DIM
        return slice(start, start + HEAD_DIM)

    for head in range(HEADS):
        queries = qkv_scr[:, part(0, head)]
        weights = softmax_rows(dot_nt(queries * FACTOR, qkv_scr[:, part(1, head)]) + bias)
        p_scr[head] = weights
        o_scr[:, part(0, head)] = dot(weights, qkv_scr[:, part(2, head)]).astype(jnp.bfloat16)
    attended = o_scr[...]
    readout = readout_ref[...]
    after = hidden + dot(attended, wout_ref[...])
    logits = jnp.sum(after * readout, axis=-1, keepdims=True)
    side = side_ref[...]
    grad_after = ((jax.nn.sigmoid(logits) - side[:, 0:1]) * side[:, 1:2]) * readout
    grad_attended = dot_nt(grad_after.astype(jnp.bfloat16), wout_ref[...]).astype(jnp.bfloat16)
    product = grad_attended.astype(jnp.float32) * attended.astype(jnp.float32)
    for head in range(HEADS):
        cols = part(0, head)
        queries = qkv_scr[:, cols]
        keys = qkv_scr[:, part(1, head)]
        values = qkv_scr[:, part(2, head)]
        grad_rows = grad_attended[:, cols]
        delta = jnp.sum(product[:, cols], axis=-1, keepdims=True)
        weights = p_scr[head]
        grad_weights = dot_nt(grad_rows, values)
        grad_scores = (
            weights.astype(jnp.float32) * ((grad_weights - delta) * FACTOR)
        ).astype(jnp.bfloat16)
        d_scr[:, cols] = dot(grad_scores, keys).astype(jnp.bfloat16)
        d_scr[:, part(1, head)] = dot_tn(grad_scores, queries).astype(jnp.bfloat16)
        d_scr[:, part(2, head)] = dot_tn(weights, grad_rows).astype(jnp.bfloat16)
    grad_normed = dot_nt(d_scr[...], win_ref[...])
    g_ref[...] = (grad_after + norm_back(hidden, inverse, gain, grad_normed)).astype(jnp.bfloat16)


def whole(*shape):
    return pl.BlockSpec(shape, lambda step: (0,) * len(shape))


def weight_specs(features):
    pairs = features // PAIR
    return [
        pl.BlockSpec((features, PAIR), lambda step: (0, step)),
        pl.BlockSpec((features, PAIR), lambda step: (0, pairs + step)),
        pl.BlockSpec((features, PAIR), lambda step: (0, 2 * pairs + step)),
        pl.BlockSpec((PAIR, features), lambda step: (step, 0)),
    ]


def space_forward(x, neighbours, gain, w_in, w_out):
    stabs, features = x.shape
    pairs = features // PAIR
    column = pl.BlockSpec((stabs, PAIR), lambda step: (0, step))
    rows = jax.ShapeDtypeStruct((stabs, features), jnp.bfloat16)
    square = pl.BlockSpec((2, stabs, stabs), lambda step: (step, 0, 0))
    return pl.pallas_call(
        space_forward_kernel,
        grid=(pairs,),
        in_specs=[whole(stabs, features), whole(*neighbours.shape), whole(1, features)]
        + weight_specs(features),
        out_specs=[whole(stabs, features), column, column, column, column, square],
        out_shape=[
            rows, rows, rows, rows, rows,
            jax.ShapeDtypeStruct((2 * pairs, stabs, stabs), jnp.bfloat16),
        ],
        scratch_shapes=[
            pltpu.VMEM((stabs, features), jnp.bfloat16),
            pltpu.VMEM((stabs, stabs), jnp.float32),
            pltpu.VMEM((stabs, features), jnp.float32),
        ],
        compiler_params=pltpu.CompilerParams(vmem_limit_bytes=VMEM_LIMIT),
        name="space_forward",
    )(x, neighbours, gain, w_in, w_in, w_in, w_out)


def space_backward(x, gain, grad, saved, w_in, w_out):
    stabs, features = x.shape
    pairs = features // PAIR
    column = pl.BlockSpec((stabs, PAIR), lambda step: (0, step))
    square = pl.BlockSpec((2, stabs, stabs), lambda step: (step, 0, 0))
    return pl.pallas_call(
        space_backward_kernel,
        grid=(pairs,),
        in_specs=[whole(stabs, features), whole(1, features), whole(stabs, features)]
        + [column] * 4
        + [square]
        + weight_specs(features),
        out_specs=whole(stabs, features),
        out_shape=jax.ShapeDtypeStruct((stabs, features), jnp.bfloat16),
        scratch_shapes=[
            pltpu.VMEM((stabs, features), jnp.float32),
            pltpu.VMEM((stabs, PAIR), jnp.bfloat16),
            pltpu.VMEM((stabs, stabs), jnp.bfloat16),
            pltpu.VMEM((stabs, PAIR), jnp.bfloat16),
            pltpu.VMEM((PAIR, stabs), jnp.bfloat16),
            pltpu.VMEM((PAIR, stabs), jnp.bfloat16),
        ],
        compiler_params=pltpu.CompilerParams(vmem_limit_bytes=VMEM_LIMIT),
        name="space_backward",
    )(x, gain, grad, *saved, w_in, w_in, w_in, w_out)


def time_both(hidden, side, gain, readout, w_in, w_out, width, tokens):
    total, features = hidden.shape
    row = pl.BlockSpec((tokens, features), lambda step: (step, 0))
    return pl.pallas_call(
        functools.partial(time_kernel, width),
        grid=(total // tokens,),
        in_specs=[
            row,
            pl.BlockSpec((tokens, 2), lambda step: (step, 0)),
            whole(1, features),
            whole(1, features),
            whole(*w_in.shape),
            whole(*w_out.shape),
        ],
        out_specs=row,
        out_shape=jax.ShapeDtypeStruct((total, features), jnp.bfloat16),
        scratch_shapes=[
            pltpu.VMEM((tokens, 3 * features), jnp.bfloat16),
            pltpu.VMEM((HEADS, tokens, tokens), jnp.bfloat16),
            pltpu.VMEM((tokens, features), jnp.bfloat16),
            pltpu.VMEM((tokens, 3 * features), jnp.bfloat16),
        ],
        compiler_params=pltpu.CompilerParams(vmem_limit_bytes=VMEM_LIMIT),
        name="time_both",
    )(hidden, side, gain, readout, w_in, w_out)


def body(
    round_size,
    stab_size,
    inputs,
    labels,
    neighbours,
    space_in_weights,
    space_out_weights,
    space_gain,
    time_in_weights,
    time_out_weights,
    time_gain,
    readout,
):
    rounds_here, stabs_here, features = inputs.shape
    rounds = rounds_here * round_size
    stabs = stabs_here * stab_size
    copies = stab_size // rounds_here
    assert copies * rounds_here == stab_size
    padded = -(-stabs_here // round_size) * round_size
    part = padded // round_size
    direct = copies == 1 and padded == stabs_here
    both = ("round", "stab")
    space_gain, time_gain, readout = space_gain[None], time_gain[None], readout[None]

    def to_rounds(tokens):
        if copies > 1:
            tokens = jnp.repeat(tokens, copies, axis=0)
        return lax.all_to_all(tokens, "stab", split_axis=0, concat_axis=1, tiled=True)[0]

    def to_tokens(rows):
        moved = lax.all_to_all(rows[None], "stab", split_axis=1, concat_axis=0, tiled=True)
        return moved[::copies] if copies > 1 else moved

    def pad_stabs(tokens):
        return jnp.pad(tokens, ((0, 0), (0, padded - stabs_here), (0, 0)))

    def to_times(rows):
        if direct:
            return lax.all_to_all(
                rows.reshape(rounds, part, features), both, split_axis=0, concat_axis=0, tiled=True
            )
        tokens = pad_stabs(to_tokens(rows))
        return lax.all_to_all(tokens, "round", split_axis=1, concat_axis=0, tiled=True)

    def from_times(times):
        if direct:
            moved = lax.all_to_all(times, both, split_axis=0, concat_axis=0, tiled=True)
            return moved.reshape(stabs, features)
        tokens = lax.all_to_all(times, "round", split_axis=0, concat_axis=1, tiled=True)
        return to_rounds(tokens[:, :stabs_here])

    here_round, here_stab = lax.axis_index("round"), lax.axis_index("stab")
    if direct:
        first = (here_round * stab_size + here_stab) * part
    else:
        first = here_stab * stabs_here + here_round * part
    slot = jnp.arange(part) + (here_round * part if not direct else 0)
    real = first + jnp.arange(part) < STABS_REAL
    if not direct:
        real = real & (slot < stabs_here)
    labels_all = lax.all_gather(labels, both, axis=0, tiled=False)
    labels_all = labels_all.reshape(round_size, stab_size, rounds_here, stabs_here)
    labels_all = jnp.transpose(labels_all, (0, 2, 1, 3)).reshape(rounds, stabs)
    labels_all = jnp.pad(labels_all, ((0, 0), (0, padded)))
    targets = lax.dynamic_slice(labels_all, (0, first), (rounds, part)).astype(jnp.float32)
    side = jnp.stack([targets, jnp.broadcast_to(real.astype(jnp.float32), targets.shape)], axis=-1)

    width = max(1, GROUP // rounds)
    while part % width:
        width -= 1
    groups = part // width
    tokens = width * rounds

    def to_groups(times):
        depth = times.shape[-1]
        split = times.reshape(rounds, groups, width, depth)
        return jnp.transpose(split, (1, 0, 2, 3)).reshape(groups * tokens, depth)

    def from_groups(rows):
        split = rows.reshape(groups, rounds, width, features)
        return jnp.transpose(split, (1, 0, 2, 3)).reshape(rounds, part, features)

    x = to_rounds(inputs)
    after_space, *saved = space_forward(
        x, neighbours, space_gain, space_in_weights, space_out_weights
    )
    times = to_groups(to_times(after_space))
    grad_times = time_both(
        times, to_groups(side), time_gain, readout, time_in_weights, time_out_weights, width, tokens
    )
    grad_space = from_times(from_groups(grad_times))
    grad = space_backward(x, space_gain, grad_space, saved, space_in_weights, space_out_weights)
    return to_tokens(grad).astype(jnp.float32)


def solution(mesh):
    in_specs = (
        P("round", "stab", None),
        P("round", "stab"),
        P(),
        P(),
        P(),
        P(),
        P(),
        P(),
        P(),
        P(),
    )
    out_specs = P("round", "stab", None)
    sized = functools.partial(body, mesh.shape["round"], mesh.shape["stab"])
    return jax.shard_map(sized, mesh=mesh, in_specs=in_specs, out_specs=out_specs, check_vma=False)
```

```python
import functools

import jax
import jax.numpy as jnp
from jax import lax
from jax.experimental import pallas as pl
from jax.experimental.pallas import tpu as pltpu
from jax.sharding import PartitionSpec as P

HEADS = 8
HEAD_DIM = 64
STABS_REAL = 840
BLOCK = 4
PAIR = 2 * HEAD_DIM
CHUNK = 448
BACK_CHUNK = 448
GROUP = 128

EPSILON = 1e-06
MASKED_SCORE = -1e30
FACTOR = HEAD_DIM ** (-0.5)
VMEM_LIMIT = 50 * 1024 * 1024


def dot(first, second):
    return jnp.dot(first, second, preferred_element_type=jnp.float32)


def dot_nt(first, second):
    return lax.dot_general(
        first, second, (((1,), (1,)), ((), ())), preferred_element_type=jnp.float32
    )


def dot_tn(first, second):
    return lax.dot_general(
        first, second, (((0,), (0,)), ((), ())), preferred_element_type=jnp.float32
    )


def inverse_rms(hidden):
    return lax.rsqrt(jnp.mean(hidden * hidden, axis=-1, keepdims=True) + EPSILON)


def norm_back(hidden, inverse, gain, upstream):
    scaled = upstream * gain
    inner = jnp.mean(hidden * scaled, axis=-1, keepdims=True)
    return inverse * scaled - hidden * (inverse * inverse * inverse * inner)


def softmax_rows(scores):
    highest = jnp.max(scores, axis=-1, keepdims=True)
    weights = jnp.exp(scores - highest)
    total = jnp.sum(weights, axis=-1, keepdims=True)
    return (weights * (1.0 / total)).astype(jnp.bfloat16)


def space_forward_kernel(
    x_ref, near_ref, gain_ref, wq_ref, wk_ref, wv_ref, wo_ref,
    h_ref, q_ref, k_ref, v_ref, o_ref, p_ref,
    n_scr, bias_scr, acc_scr,
):
    step = pl.program_id(0)
    stabs = x_ref.shape[0]
    blocks, links = near_ref.shape

    @pl.when(step == 0)
    def _():
        x = x_ref[...].astype(jnp.float32)
        n_scr[...] = (x * inverse_rms(x) * gain_ref[...]).astype(jnp.bfloat16)
        acc_scr[...] = x
        lanes = lax.broadcasted_iota(jnp.int32, (blocks, blocks), 1)
        near = near_ref[...]
        listed = jnp.zeros((blocks, blocks), jnp.float32)
        for link in range(links):
            listed = jnp.where(lanes == near[:, link : link + 1], 1.0, listed)
        owner = lax.broadcasted_iota(jnp.int32, (stabs, blocks), 0) // BLOCK
        column = lax.broadcasted_iota(jnp.int32, (stabs, blocks), 1)
        widen = jnp.where(owner == column, 1.0, 0.0).astype(jnp.bfloat16)
        rows = dot(widen, listed.astype(jnp.bfloat16)).astype(jnp.bfloat16)
        bias_scr[...] = jnp.where(dot_nt(rows, widen) > 0.5, 0.0, MASKED_SCORE)

    n = n_scr[...]
    q_ref[...] = dot(n, wq_ref[...]).astype(jnp.bfloat16)
    k_ref[...] = dot(n, wk_ref[...]).astype(jnp.bfloat16)
    v_ref[...] = dot(n, wv_ref[...]).astype(jnp.bfloat16)
    for head in range(2):
        cols = slice(head * HEAD_DIM, (head + 1) * HEAD_DIM)
        keys = k_ref[:, cols]
        values = v_ref[:, cols]
        for start in range(0, stabs, CHUNK):
            rows = slice(start, start + CHUNK)
            scores = dot_nt(q_ref[rows, cols] * FACTOR, keys) + bias_scr[rows, :]
            weights = softmax_rows(scores)
            p_ref[head, rows, :] = weights
            o_ref[rows, cols] = dot(weights, values).astype(jnp.bfloat16)
    acc_scr[...] += dot(o_ref[...], wo_ref[...])

    @pl.when(step == pl.num_programs(0) - 1)
    def _():
        h_ref[...] = acc_scr[...].astype(jnp.bfloat16)


def space_backward_kernel(
    x_ref, gain_ref, g_ref, q_ref, k_ref, v_ref, o_ref, p_ref,
    wq_ref, wk_ref, wv_ref, wo_ref,
    out_ref,
    gn_scr, go_scr, gs_scr, dq_scr, dk_scr, dv_scr,
):
    step = pl.program_id(0)
    stabs = x_ref.shape[0]
    go = dot_nt(g_ref[...], wo_ref[...]).astype(jnp.bfloat16)
    go_scr[...] = go
    product = go.astype(jnp.float32) * o_ref[...].astype(jnp.float32)
    q_turned = q_ref[...].T
    go_turned = go.T
    for head in range(2):
        cols = slice(head * HEAD_DIM, (head + 1) * HEAD_DIM)
        keys = k_ref[:, cols]
        values = v_ref[:, cols]
        delta = jnp.sum(product[:, cols], axis=-1, keepdims=True)
        for start in range(0, stabs, BACK_CHUNK):
            rows = slice(start, start + BACK_CHUNK)
            grad_weights = dot_nt(go_scr[rows, cols], values)
            weights = p_ref[head, rows, :].astype(jnp.float32)
            grad_scores = (
                weights * ((grad_weights - delta[start : start + BACK_CHUNK]) * FACTOR)
            ).astype(jnp.bfloat16)
            gs_scr[rows, :] = grad_scores
            dq_scr[rows, cols] = dot(grad_scores, keys).astype(jnp.bfloat16)
        dk_scr[cols, :] = dot(q_turned[cols, :], gs_scr[...]).astype(jnp.bfloat16)
        dv_scr[cols, :] = dot(go_turned[cols, :], p_ref[head]).astype(jnp.bfloat16)
    part = (
        dot_nt(dq_scr[...], wq_ref[...])
        + dot_nt(dk_scr[...].T, wk_ref[...])
        + dot_nt(dv_scr[...].T, wv_ref[...])
    )

    @pl.when(step == 0)
    def _():
        gn_scr[...] = part

    @pl.when(step > 0)
    def _():
        gn_scr[...] += part

    @pl.when(step == pl.num_programs(0) - 1)
    def _():
        x = x_ref[...].astype(jnp.float32)
        back = norm_back(x, inverse_rms(x), gain_ref[...], gn_scr[...])
        out_ref[...] = (g_ref[...].astype(jnp.float32) + back).astype(jnp.bfloat16)


def time_kernel(
    width, h_ref, side_ref, gain_ref, readout_ref, win_ref, wout_ref,
    g_ref,
    qkv_scr, p_scr, o_scr, go_scr, d_scr,
):
    total, features = h_ref.shape
    tokens = p_scr.shape[-1]
    groups = total // tokens
    hidden = h_ref[...].astype(jnp.float32)
    inverse = inverse_rms(hidden)
    gain = gain_ref[...]
    normed = (hidden * inverse * gain).astype(jnp.bfloat16)
    qkv_scr[...] = dot(normed, win_ref[...]).astype(jnp.bfloat16)
    left = lax.broadcasted_iota(jnp.int32, (tokens, tokens), 0)
    right = lax.broadcasted_iota(jnp.int32, (tokens, tokens), 1)
    kept = ((left % width) == (right % width)) & (right <= left)
    bias = jnp.where(kept, 0.0, MASKED_SCORE)
    bias = jnp.concatenate([bias, bias], axis=0)

    pairs = features // PAIR
    lanes = lax.broadcasted_iota(jnp.int32, (tokens, PAIR), 1)
    near = lanes < HEAD_DIM

    def part(index, pair):
        start = index * features + pair * PAIR
        return slice(start, start + PAIR)

    def rows_of(group):
        return pl.ds(pl.multiple_of(group * tokens, tokens), tokens)

    def stacked(block):
        empty = jnp.zeros_like(block)
        return jnp.concatenate(
            [jnp.where(near, block, empty), jnp.where(near, empty, block)], axis=0
        )

    def merged(block):
        return jnp.where(near, block[:tokens], block[tokens:]).astype(jnp.bfloat16)

    def ahead(group, carry):
        rows = rows_of(group)
        scores = [
            dot_nt(stacked(qkv_scr[rows, part(0, pair)] * FACTOR), qkv_scr[rows, part(1, pair)])
            for pair in range(pairs)
        ]
        weights = [softmax_rows(score + bias) for score in scores]
        for pair in range(pairs):
            p_scr[group * pairs + pair] = weights[pair]
        outs = [dot(weights[pair], qkv_scr[rows, part(2, pair)]) for pair in range(pairs)]
        for pair in range(pairs):
            o_scr[rows, part(0, pair)] = merged(outs[pair])
        return carry

    lax.fori_loop(0, groups, ahead, 0)
    readout = readout_ref[...]
    after = hidden + dot(o_scr[...], wout_ref[...])
    logits = jnp.sum(after * readout, axis=-1, keepdims=True)
    side = side_ref[...]
    grad_logits = (jax.nn.sigmoid(logits) - side[:, 0:1]) * side[:, 1:2]
    grad_after = grad_logits * readout
    go_scr[...] = dot_nt(grad_after.astype(jnp.bfloat16), wout_ref[...]).astype(jnp.bfloat16)

    def behind(group, carry):
        rows = rows_of(group)
        span = range(pairs)
        upstream = [stacked(go_scr[rows, part(0, pair)]) for pair in span]
        products = [dot_nt(upstream[pair], qkv_scr[rows, part(2, pair)]) for pair in span]
        weights = [p_scr[group * pairs + pair] for pair in span]
        grad_scores = []
        for pair in span:
            attended = o_scr[rows, part(0, pair)].astype(jnp.float32)
            attended = jnp.concatenate([attended, attended], axis=0)
            delta = jnp.sum(
                upstream[pair].astype(jnp.float32) * attended, axis=-1, keepdims=True
            )
            grad_scores.append(
                (weights[pair].astype(jnp.float32) * ((products[pair] - delta) * FACTOR)).astype(
                    jnp.bfloat16
                )
            )
        queries = [dot(grad_scores[pair], qkv_scr[rows, part(1, pair)]) for pair in span]
        keys = [dot_tn(grad_scores[pair], stacked(qkv_scr[rows, part(0, pair)])) for pair in span]
        values = [dot_tn(weights[pair], upstream[pair]) for pair in span]
        for pair in span:
            d_scr[rows, part(0, pair)] = merged(queries[pair])
            d_scr[rows, part(1, pair)] = keys[pair].astype(jnp.bfloat16)
            d_scr[rows, part(2, pair)] = values[pair].astype(jnp.bfloat16)
        return carry

    lax.fori_loop(0, groups, behind, 0)
    grad_normed = dot_nt(d_scr[...], win_ref[...])
    hidden = h_ref[...].astype(jnp.float32)
    back = norm_back(hidden, inverse, gain, grad_normed)
    g_ref[...] = (grad_logits * readout + back).astype(jnp.bfloat16)


def whole(*shape):
    return pl.BlockSpec(shape, lambda step: (0,) * len(shape))


def weight_specs(features):
    pairs = features // PAIR
    return [
        pl.BlockSpec((features, PAIR), lambda step: (0, step)),
        pl.BlockSpec((features, PAIR), lambda step: (0, pairs + step)),
        pl.BlockSpec((features, PAIR), lambda step: (0, 2 * pairs + step)),
        pl.BlockSpec((PAIR, features), lambda step: (step, 0)),
    ]


def space_forward(x, neighbours, gain, w_in, w_out):
    stabs, features = x.shape
    pairs = features // PAIR
    column = pl.BlockSpec((stabs, PAIR), lambda step: (0, step))
    rows = jax.ShapeDtypeStruct((stabs, features), jnp.bfloat16)
    square = pl.BlockSpec((2, stabs, stabs), lambda step: (step, 0, 0))
    return pl.pallas_call(
        space_forward_kernel,
        grid=(pairs,),
        in_specs=[whole(stabs, features), whole(*neighbours.shape), whole(1, features)]
        + weight_specs(features),
        out_specs=[whole(stabs, features), column, column, column, column, square],
        out_shape=[
            rows, rows, rows, rows, rows,
            jax.ShapeDtypeStruct((2 * pairs, stabs, stabs), jnp.bfloat16),
        ],
        scratch_shapes=[
            pltpu.VMEM((stabs, features), jnp.bfloat16),
            pltpu.VMEM((stabs, stabs), jnp.float32),
            pltpu.VMEM((stabs, features), jnp.float32),
        ],
        compiler_params=pltpu.CompilerParams(vmem_limit_bytes=VMEM_LIMIT),
        name="space_forward",
    )(x, neighbours, gain, w_in, w_in, w_in, w_out)


def space_backward(x, gain, grad, saved, w_in, w_out):
    stabs, features = x.shape
    pairs = features // PAIR
    column = pl.BlockSpec((stabs, PAIR), lambda step: (0, step))
    square = pl.BlockSpec((2, stabs, stabs), lambda step: (step, 0, 0))
    return pl.pallas_call(
        space_backward_kernel,
        grid=(pairs,),
        in_specs=[whole(stabs, features), whole(1, features), whole(stabs, features)]
        + [column] * 4
        + [square]
        + weight_specs(features),
        out_specs=whole(stabs, features),
        out_shape=jax.ShapeDtypeStruct((stabs, features), jnp.bfloat16),
        scratch_shapes=[
            pltpu.VMEM((stabs, features), jnp.float32),
            pltpu.VMEM((stabs, PAIR), jnp.bfloat16),
            pltpu.VMEM((stabs, stabs), jnp.bfloat16),
            pltpu.VMEM((stabs, PAIR), jnp.bfloat16),
            pltpu.VMEM((PAIR, stabs), jnp.bfloat16),
            pltpu.VMEM((PAIR, stabs), jnp.bfloat16),
        ],
        compiler_params=pltpu.CompilerParams(vmem_limit_bytes=VMEM_LIMIT),
        name="space_backward",
    )(x, gain, grad, *saved, w_in, w_in, w_in, w_out)


def time_both(hidden, side, gain, readout, w_in, w_out, width, tokens):
    total, features = hidden.shape
    return pl.pallas_call(
        functools.partial(time_kernel, width),
        out_shape=jax.ShapeDtypeStruct((total, features), jnp.bfloat16),
        scratch_shapes=[
            pltpu.VMEM((total, 3 * features), jnp.bfloat16),
            pltpu.VMEM((total // tokens * (features // PAIR), 2 * tokens, tokens), jnp.bfloat16),
            pltpu.VMEM((total, features), jnp.bfloat16),
            pltpu.VMEM((total, features), jnp.bfloat16),
            pltpu.VMEM((total, 3 * features), jnp.bfloat16),
        ],
        compiler_params=pltpu.CompilerParams(vmem_limit_bytes=VMEM_LIMIT),
        name="time_both",
    )(hidden, side, gain, readout, w_in, w_out)


def body(
    round_size,
    stab_size,
    inputs,
    labels,
    neighbours,
    space_in_weights,
    space_out_weights,
    space_gain,
    time_in_weights,
    time_out_weights,
    time_gain,
    readout,
):
    rounds_here, stabs_here, features = inputs.shape
    rounds = rounds_here * round_size
    stabs = stabs_here * stab_size
    copies = stab_size // rounds_here
    assert copies * rounds_here == stab_size
    padded = -(-stabs_here // round_size) * round_size
    part = padded // round_size
    direct = copies == 1 and padded == stabs_here
    both = ("round", "stab")
    space_gain, time_gain, readout = space_gain[None], time_gain[None], readout[None]

    def to_rounds(tokens):
        if copies > 1:
            tokens = jnp.repeat(tokens, copies, axis=0)
        return lax.all_to_all(tokens, "stab", split_axis=0, concat_axis=1, tiled=True)[0]

    def to_tokens(rows):
        split = rows.reshape(stab_size, stabs_here, features)
        moved = lax.all_to_all(split, "stab", split_axis=0, concat_axis=0, tiled=True)
        return moved[::copies] if copies > 1 else moved

    def pad_stabs(tokens):
        return jnp.pad(tokens, ((0, 0), (0, padded - stabs_here), (0, 0)))

    def to_times(rows):
        if direct:
            return lax.all_to_all(
                rows.reshape(rounds, part, features), both, split_axis=0, concat_axis=0, tiled=True
            )
        tokens = pad_stabs(to_tokens(rows))
        return lax.all_to_all(tokens, "round", split_axis=1, concat_axis=0, tiled=True)

    def from_times(times):
        if direct:
            moved = lax.all_to_all(times, both, split_axis=0, concat_axis=0, tiled=True)
            return moved.reshape(stabs, features)
        tokens = lax.all_to_all(times, "round", split_axis=0, concat_axis=1, tiled=True)
        return to_rounds(tokens[:, :stabs_here])

    here_round, here_stab = lax.axis_index("round"), lax.axis_index("stab")
    if direct:
        first = (here_round * stab_size + here_stab) * part
        chunks = jnp.transpose(labels.reshape(rounds_here, round_size, part), (1, 0, 2))
        sent = jnp.tile(chunks.reshape(round_size, rounds_here * part), (stab_size, 1))
        came = lax.all_to_all(sent, both, split_axis=0, concat_axis=0, tiled=True)
        came = came.reshape(round_size, stab_size, rounds_here, part)
        owner = (here_round * stab_size + here_stab) // round_size
        targets = lax.dynamic_index_in_dim(came, owner, 1, keepdims=False)
        targets = targets.reshape(rounds, part).astype(jnp.float32)
    else:
        first = here_stab * stabs_here + here_round * part
        labels_all = lax.all_gather(labels, both, axis=0, tiled=False)
        labels_all = labels_all.reshape(round_size, stab_size, rounds_here, stabs_here)
        labels_all = jnp.transpose(labels_all, (0, 2, 1, 3)).reshape(rounds, stabs)
        labels_all = jnp.pad(labels_all, ((0, 0), (0, padded)))
        targets = lax.dynamic_slice(labels_all, (0, first), (rounds, part)).astype(jnp.float32)
    slot = jnp.arange(part) + (here_round * part if not direct else 0)
    real = first + jnp.arange(part) < STABS_REAL
    if not direct:
        real = real & (slot < stabs_here)
    side = jnp.stack([targets, jnp.broadcast_to(real.astype(jnp.float32), targets.shape)], axis=-1)

    width = max(1, GROUP // rounds)
    while part % width:
        width -= 1
    groups = part // width
    tokens = width * rounds

    def to_groups(times):
        depth = times.shape[-1]
        split = times.reshape(rounds, groups, width, depth)
        return jnp.transpose(split, (1, 0, 2, 3)).reshape(groups * tokens, depth)

    def from_groups(rows):
        split = rows.reshape(groups, rounds, width, features)
        return jnp.transpose(split, (1, 0, 2, 3)).reshape(rounds, part, features)

    x = to_rounds(inputs)
    after_space, *saved = space_forward(
        x, neighbours, space_gain, space_in_weights, space_out_weights
    )
    times = to_groups(to_times(after_space))
    grad_times = time_both(
        times, to_groups(side), time_gain, readout, time_in_weights, time_out_weights, width, tokens
    )
    grad_space = from_times(from_groups(grad_times))
    grad = space_backward(x, space_gain, grad_space, saved, space_in_weights, space_out_weights)
    return to_tokens(grad).astype(jnp.float32)


def solution(mesh):
    in_specs = (
        P("round", "stab", None),
        P("round", "stab"),
        P(),
        P(),
        P(),
        P(),
        P(),
        P(),
        P(),
        P(),
    )
    out_specs = P("round", "stab", None)
    sized = functools.partial(body, mesh.shape["round"], mesh.shape["stab"])
    return jax.shard_map(sized, mesh=mesh, in_specs=in_specs, out_specs=out_specs, check_vma=False)
```

```python
import functools

import jax
import jax.numpy as jnp
from jax import lax
from jax.experimental import pallas as pl
from jax.experimental.pallas import tpu as pltpu
from jax.sharding import PartitionSpec as P

HEADS = 8
HEAD_DIM = 64
STABS_REAL = 840
BLOCK = 4
PAIR = 2 * HEAD_DIM
CHUNK = 448
BACK_CHUNK = 448
GROUP = 128

EPSILON = 1e-06
MASKED_SCORE = -1e30
FACTOR = HEAD_DIM ** (-0.5)
VMEM_LIMIT = 50 * 1024 * 1024


def dot(first, second):
    return jnp.dot(first, second, preferred_element_type=jnp.float32)


def dot_nt(first, second):
    return lax.dot_general(
        first, second, (((1,), (1,)), ((), ())), preferred_element_type=jnp.float32
    )


def dot_tn(first, second):
    return lax.dot_general(
        first, second, (((0,), (0,)), ((), ())), preferred_element_type=jnp.float32
    )


def inverse_rms(hidden):
    return lax.rsqrt(jnp.mean(hidden * hidden, axis=-1, keepdims=True) + EPSILON)


def norm_back(hidden, inverse, gain, upstream):
    scaled = upstream * gain
    inner = jnp.mean(hidden * scaled, axis=-1, keepdims=True)
    return inverse * scaled - hidden * (inverse * inverse * inverse * inner)


def softmax_rows(scores):
    highest = jnp.max(scores, axis=-1, keepdims=True)
    weights = jnp.exp(scores - highest)
    total = jnp.sum(weights, axis=-1, keepdims=True)
    return (weights * (1.0 / total)).astype(jnp.bfloat16)


def space_forward_kernel(
    x_ref, near_ref, gain_ref, wq_ref, wk_ref, wv_ref, wo_ref,
    h_ref, q_ref, k_ref, v_ref, o_ref, p_ref,
    n_scr, bias_scr, acc_scr,
):
    step = pl.program_id(0)
    stabs = x_ref.shape[0]
    blocks, links = near_ref.shape

    @pl.when(step == 0)
    def _():
        x = x_ref[...].astype(jnp.float32)
        n_scr[...] = (x * inverse_rms(x) * gain_ref[...]).astype(jnp.bfloat16)
        acc_scr[...] = x
        lanes = lax.broadcasted_iota(jnp.int32, (blocks, blocks), 1)
        near = near_ref[...]
        listed = jnp.zeros((blocks, blocks), jnp.float32)
        for link in range(links):
            listed = jnp.where(lanes == near[:, link : link + 1], 1.0, listed)
        owner = lax.broadcasted_iota(jnp.int32, (stabs, blocks), 0) // BLOCK
        column = lax.broadcasted_iota(jnp.int32, (stabs, blocks), 1)
        widen = jnp.where(owner == column, 1.0, 0.0).astype(jnp.bfloat16)
        rows = dot(widen, listed.astype(jnp.bfloat16)).astype(jnp.bfloat16)
        bias_scr[...] = jnp.where(dot_nt(rows, widen) > 0.5, 0.0, MASKED_SCORE)

    n = n_scr[...]
    q_ref[...] = dot(n, wq_ref[...]).astype(jnp.bfloat16)
    k_ref[...] = dot(n, wk_ref[...]).astype(jnp.bfloat16)
    v_ref[...] = dot(n, wv_ref[...]).astype(jnp.bfloat16)
    for head in range(2):
        cols = slice(head * HEAD_DIM, (head + 1) * HEAD_DIM)
        keys = k_ref[:, cols]
        values = v_ref[:, cols]
        for start in range(0, stabs, CHUNK):
            rows = slice(start, start + CHUNK)
            scores = dot_nt(q_ref[rows, cols] * FACTOR, keys) + bias_scr[rows, :]
            weights = softmax_rows(scores)
            p_ref[head, rows, :] = weights
            o_ref[rows, cols] = dot(weights, values).astype(jnp.bfloat16)
    acc_scr[...] += dot(o_ref[...], wo_ref[...])

    @pl.when(step == pl.num_programs(0) - 1)
    def _():
        h_ref[...] = acc_scr[...].astype(jnp.bfloat16)


def space_backward_kernel(
    x_ref, gain_ref, g_ref, q_ref, k_ref, v_ref, o_ref, p_ref,
    wq_ref, wk_ref, wv_ref, wo_ref,
    out_ref,
    gn_scr, go_scr, gs_scr, dq_scr, dk_scr, dv_scr,
):
    step = pl.program_id(0)
    stabs = x_ref.shape[0]
    go = dot_nt(g_ref[...], wo_ref[...]).astype(jnp.bfloat16)
    go_scr[...] = go
    product = go.astype(jnp.float32) * o_ref[...].astype(jnp.float32)
    q_turned = q_ref[...].T
    go_turned = go.T
    for head in range(2):
        cols = slice(head * HEAD_DIM, (head + 1) * HEAD_DIM)
        keys = k_ref[:, cols]
        values = v_ref[:, cols]
        delta = jnp.sum(product[:, cols], axis=-1, keepdims=True)
        for start in range(0, stabs, BACK_CHUNK):
            rows = slice(start, start + BACK_CHUNK)
            grad_weights = dot_nt(go_scr[rows, cols], values)
            weights = p_ref[head, rows, :].astype(jnp.float32)
            grad_scores = (
                weights * ((grad_weights - delta[start : start + BACK_CHUNK]) * FACTOR)
            ).astype(jnp.bfloat16)
            gs_scr[rows, :] = grad_scores
            dq_scr[rows, cols] = dot(grad_scores, keys).astype(jnp.bfloat16)
        dk_scr[cols, :] = dot(q_turned[cols, :], gs_scr[...]).astype(jnp.bfloat16)
        dv_scr[cols, :] = dot(go_turned[cols, :], p_ref[head]).astype(jnp.bfloat16)
    part = (
        dot_nt(dq_scr[...], wq_ref[...])
        + dot_nt(dk_scr[...].T, wk_ref[...])
        + dot_nt(dv_scr[...].T, wv_ref[...])
    )

    @pl.when(step == 0)
    def _():
        gn_scr[...] = part

    @pl.when(step > 0)
    def _():
        gn_scr[...] += part

    @pl.when(step == pl.num_programs(0) - 1)
    def _():
        x = x_ref[...].astype(jnp.float32)
        back = norm_back(x, inverse_rms(x), gain_ref[...], gn_scr[...])
        out_ref[...] = (g_ref[...].astype(jnp.float32) + back).astype(jnp.bfloat16)


def time_kernel(
    width, h_ref, side_ref, gain_ref, readout_ref, win_ref, wout_ref,
    g_ref,
    qkv_scr, p_scr, o_scr, go_scr, d_scr,
):
    total, features = h_ref.shape
    tokens = p_scr.shape[-1]
    groups = total // tokens
    hidden = h_ref[...].astype(jnp.float32)
    inverse = inverse_rms(hidden)
    gain = gain_ref[...]
    normed = (hidden * inverse * gain).astype(jnp.bfloat16)
    qkv_scr[...] = dot(normed, win_ref[...]).astype(jnp.bfloat16)
    left = lax.broadcasted_iota(jnp.int32, (tokens, tokens), 0)
    right = lax.broadcasted_iota(jnp.int32, (tokens, tokens), 1)
    kept = ((left % width) == (right % width)) & (right <= left)
    bias = jnp.where(kept, 0.0, MASKED_SCORE)
    bias = jnp.concatenate([bias, bias], axis=0)

    pairs = features // PAIR
    lanes = lax.broadcasted_iota(jnp.int32, (tokens, PAIR), 1)
    near = lanes < HEAD_DIM

    def part(index, pair):
        start = index * features + pair * PAIR
        return slice(start, start + PAIR)

    def rows_of(group):
        return pl.ds(pl.multiple_of(group * tokens, tokens), tokens)

    def stacked(block):
        empty = jnp.zeros_like(block)
        return jnp.concatenate(
            [jnp.where(near, block, empty), jnp.where(near, empty, block)], axis=0
        )

    def merged(block):
        return jnp.where(near, block[:tokens], block[tokens:]).astype(jnp.bfloat16)

    def ahead(group, carry):
        rows = rows_of(group)
        scores = [
            dot_nt(stacked(qkv_scr[rows, part(0, pair)] * FACTOR), qkv_scr[rows, part(1, pair)])
            for pair in range(pairs)
        ]
        weights = [softmax_rows(score + bias) for score in scores]
        for pair in range(pairs):
            p_scr[group * pairs + pair] = weights[pair]
        outs = [dot(weights[pair], qkv_scr[rows, part(2, pair)]) for pair in range(pairs)]
        for pair in range(pairs):
            o_scr[rows, part(0, pair)] = merged(outs[pair])
        return carry

    lax.fori_loop(0, groups, ahead, 0)
    readout = readout_ref[...]
    after = hidden + dot(o_scr[...], wout_ref[...])
    logits = jnp.sum(after * readout, axis=-1, keepdims=True)
    side = side_ref[...]
    grad_logits = (jax.nn.sigmoid(logits) - side[:, 0:1]) * side[:, 1:2]
    grad_after = grad_logits * readout
    go_scr[...] = dot_nt(grad_after.astype(jnp.bfloat16), wout_ref[...]).astype(jnp.bfloat16)

    def behind(group, carry):
        rows = rows_of(group)
        span = range(pairs)
        upstream = [stacked(go_scr[rows, part(0, pair)]) for pair in span]
        products = [dot_nt(upstream[pair], qkv_scr[rows, part(2, pair)]) for pair in span]
        weights = [p_scr[group * pairs + pair] for pair in span]
        grad_scores = []
        for pair in span:
            attended = o_scr[rows, part(0, pair)].astype(jnp.float32)
            attended = jnp.concatenate([attended, attended], axis=0)
            delta = jnp.sum(
                upstream[pair].astype(jnp.float32) * attended, axis=-1, keepdims=True
            )
            grad_scores.append(
                (weights[pair].astype(jnp.float32) * ((products[pair] - delta) * FACTOR)).astype(
                    jnp.bfloat16
                )
            )
        queries = [dot(grad_scores[pair], qkv_scr[rows, part(1, pair)]) for pair in span]
        keys = [dot_tn(grad_scores[pair], stacked(qkv_scr[rows, part(0, pair)])) for pair in span]
        values = [dot_tn(weights[pair], upstream[pair]) for pair in span]
        for pair in span:
            d_scr[rows, part(0, pair)] = merged(queries[pair])
            d_scr[rows, part(1, pair)] = keys[pair].astype(jnp.bfloat16)
            d_scr[rows, part(2, pair)] = values[pair].astype(jnp.bfloat16)
        return carry

    lax.fori_loop(0, groups, behind, 0)
    grad_normed = dot_nt(d_scr[...], win_ref[...])
    hidden = h_ref[...].astype(jnp.float32)
    back = norm_back(hidden, inverse, gain, grad_normed)
    g_ref[...] = (grad_logits * readout + back).astype(jnp.bfloat16)


def whole(*shape):
    return pl.BlockSpec(shape, lambda step: (0,) * len(shape))


def weight_specs(features):
    pairs = features // PAIR
    return [
        pl.BlockSpec((features, PAIR), lambda step: (0, step)),
        pl.BlockSpec((features, PAIR), lambda step: (0, pairs + step)),
        pl.BlockSpec((features, PAIR), lambda step: (0, 2 * pairs + step)),
        pl.BlockSpec((PAIR, features), lambda step: (step, 0)),
    ]


def space_forward(x, neighbours, gain, w_in, w_out):
    stabs, features = x.shape
    pairs = features // PAIR
    column = pl.BlockSpec((stabs, PAIR), lambda step: (0, step))
    rows = jax.ShapeDtypeStruct((stabs, features), jnp.bfloat16)
    square = pl.BlockSpec((2, stabs, stabs), lambda step: (step, 0, 0))
    return pl.pallas_call(
        space_forward_kernel,
        grid=(pairs,),
        in_specs=[whole(stabs, features), whole(*neighbours.shape), whole(1, features)]
        + weight_specs(features),
        out_specs=[whole(stabs, features), column, column, column, column, square],
        out_shape=[
            rows, rows, rows, rows, rows,
            jax.ShapeDtypeStruct((2 * pairs, stabs, stabs), jnp.bfloat16),
        ],
        scratch_shapes=[
            pltpu.VMEM((stabs, features), jnp.bfloat16),
            pltpu.VMEM((stabs, stabs), jnp.float32),
            pltpu.VMEM((stabs, features), jnp.float32),
        ],
        compiler_params=pltpu.CompilerParams(vmem_limit_bytes=VMEM_LIMIT),
        name="space_forward",
    )(x, neighbours, gain, w_in, w_in, w_in, w_out)


def space_backward(x, gain, grad, saved, w_in, w_out):
    stabs, features = x.shape
    pairs = features // PAIR
    column = pl.BlockSpec((stabs, PAIR), lambda step: (0, step))
    square = pl.BlockSpec((2, stabs, stabs), lambda step: (step, 0, 0))
    return pl.pallas_call(
        space_backward_kernel,
        grid=(pairs,),
        in_specs=[whole(stabs, features), whole(1, features), whole(stabs, features)]
        + [column] * 4
        + [square]
        + weight_specs(features),
        out_specs=whole(stabs, features),
        out_shape=jax.ShapeDtypeStruct((stabs, features), jnp.bfloat16),
        scratch_shapes=[
            pltpu.VMEM((stabs, features), jnp.float32),
            pltpu.VMEM((stabs, PAIR), jnp.bfloat16),
            pltpu.VMEM((stabs, stabs), jnp.bfloat16),
            pltpu.VMEM((stabs, PAIR), jnp.bfloat16),
            pltpu.VMEM((PAIR, stabs), jnp.bfloat16),
            pltpu.VMEM((PAIR, stabs), jnp.bfloat16),
        ],
        compiler_params=pltpu.CompilerParams(vmem_limit_bytes=VMEM_LIMIT),
        name="space_backward",
    )(x, gain, grad, *saved, w_in, w_in, w_in, w_out)


def time_both(hidden, side, gain, readout, w_in, w_out, width, tokens):
    total, features = hidden.shape
    return pl.pallas_call(
        functools.partial(time_kernel, width),
        out_shape=jax.ShapeDtypeStruct((total, features), jnp.bfloat16),
        scratch_shapes=[
            pltpu.VMEM((total, 3 * features), jnp.bfloat16),
            pltpu.VMEM((total // tokens * (features // PAIR), 2 * tokens, tokens), jnp.bfloat16),
            pltpu.VMEM((total, features), jnp.bfloat16),
            pltpu.VMEM((total, features), jnp.bfloat16),
            pltpu.VMEM((total, 3 * features), jnp.bfloat16),
        ],
        compiler_params=pltpu.CompilerParams(vmem_limit_bytes=VMEM_LIMIT),
        name="time_both",
    )(hidden, side, gain, readout, w_in, w_out)


def body(
    round_size,
    stab_size,
    inputs,
    labels,
    neighbours,
    space_in_weights,
    space_out_weights,
    space_gain,
    time_in_weights,
    time_out_weights,
    time_gain,
    readout,
):
    rounds_here, stabs_here, features = inputs.shape
    rounds = rounds_here * round_size
    stabs = stabs_here * stab_size
    copies = stab_size // rounds_here
    assert copies * rounds_here == stab_size
    padded = -(-stabs_here // round_size) * round_size
    part = padded // round_size
    direct = copies == 1 and padded == stabs_here
    both = ("round", "stab")
    space_gain, time_gain, readout = space_gain[None], time_gain[None], readout[None]

    def to_rounds(tokens):
        if copies > 1:
            tokens = jnp.repeat(tokens, copies, axis=0)
        return lax.all_to_all(tokens, "stab", split_axis=0, concat_axis=1, tiled=True)[0]

    def to_tokens(rows):
        split = rows.reshape(stab_size, stabs_here, features)
        moved = lax.all_to_all(split, "stab", split_axis=0, concat_axis=0, tiled=True)
        return moved[::copies] if copies > 1 else moved

    def pad_stabs(tokens):
        return jnp.pad(tokens, ((0, 0), (0, padded - stabs_here), (0, 0)))

    def to_times(rows):
        if direct:
            split = rows.reshape(rounds, part, features)
            return [
                lax.all_to_all(split[:, piece], both, split_axis=0, concat_axis=0, tiled=True)
                for piece in pieces
            ]
        tokens = pad_stabs(to_tokens(rows))
        return [lax.all_to_all(tokens, "round", split_axis=1, concat_axis=0, tiled=True)]

    def from_times(times):
        if direct:
            moved = [
                lax.all_to_all(piece, both, split_axis=0, concat_axis=0, tiled=True)
                for piece in times
            ]
            return jnp.concatenate(moved, axis=1).reshape(stabs, features)
        tokens = lax.all_to_all(times[0], "round", split_axis=0, concat_axis=1, tiled=True)
        return to_rounds(tokens[:, :stabs_here])

    width = max(1, GROUP // rounds)
    while part % width:
        width -= 1
    tokens = width * rounds
    pieces = [slice(0, part)]
    if direct and part > width:
        middle = -(-part // (2 * width)) * width
        pieces = [slice(0, middle), slice(middle, part)]

    here_round, here_stab = lax.axis_index("round"), lax.axis_index("stab")
    if direct:
        first = (here_round * stab_size + here_stab) * part
        chunks = jnp.transpose(labels.reshape(rounds_here, round_size, part), (1, 0, 2))
        sent = jnp.tile(chunks.reshape(round_size, rounds_here * part), (stab_size, 1))
        came = lax.all_to_all(sent, both, split_axis=0, concat_axis=0, tiled=True)
        came = came.reshape(round_size, stab_size, rounds_here, part)
        owner = (here_round * stab_size + here_stab) // round_size
        targets = lax.dynamic_index_in_dim(came, owner, 1, keepdims=False)
        targets = targets.reshape(rounds, part).astype(jnp.float32)
    else:
        first = here_stab * stabs_here + here_round * part
        labels_all = lax.all_gather(labels, both, axis=0, tiled=False)
        labels_all = labels_all.reshape(round_size, stab_size, rounds_here, stabs_here)
        labels_all = jnp.transpose(labels_all, (0, 2, 1, 3)).reshape(rounds, stabs)
        labels_all = jnp.pad(labels_all, ((0, 0), (0, padded)))
        targets = lax.dynamic_slice(labels_all, (0, first), (rounds, part)).astype(jnp.float32)
    slot = jnp.arange(part) + (here_round * part if not direct else 0)
    real = first + jnp.arange(part) < STABS_REAL
    if not direct:
        real = real & (slot < stabs_here)
    side = jnp.stack([targets, jnp.broadcast_to(real.astype(jnp.float32), targets.shape)], axis=-1)

    def to_groups(times):
        depth = times.shape[-1]
        split = times.reshape(rounds, -1, width, depth)
        return jnp.transpose(split, (1, 0, 2, 3)).reshape(-1, depth)

    def from_groups(rows):
        split = rows.reshape(-1, rounds, width, features)
        return jnp.transpose(split, (1, 0, 2, 3)).reshape(rounds, -1, features)

    x = to_rounds(inputs)
    after_space, *saved = space_forward(
        x, neighbours, space_gain, space_in_weights, space_out_weights
    )
    grad_times = [
        from_groups(
            time_both(
                to_groups(times), to_groups(side[:, piece]), time_gain, readout,
                time_in_weights, time_out_weights, width, tokens,
            )
        )
        for times, piece in zip(to_times(after_space), pieces)
    ]
    grad_space = from_times(grad_times)
    grad = space_backward(x, space_gain, grad_space, saved, space_in_weights, space_out_weights)
    return to_tokens(grad).astype(jnp.float32)


def solution(mesh):
    in_specs = (
        P("round", "stab", None),
        P("round", "stab"),
        P(),
        P(),
        P(),
        P(),
        P(),
        P(),
        P(),
        P(),
    )
    out_specs = P("round", "stab", None)
    sized = functools.partial(body, mesh.shape["round"], mesh.shape["stab"])
    return jax.shard_map(sized, mesh=mesh, in_specs=in_specs, out_specs=out_specs, check_vma=False)
```

```python
import functools

import jax
import jax.numpy as jnp
from jax import lax
from jax.experimental import pallas as pl
from jax.experimental.pallas import tpu as pltpu
from jax.sharding import PartitionSpec as P

HEADS = 8
HEAD_DIM = 64
STABS_REAL = 840
BLOCK = 4
PAIR = 2 * HEAD_DIM
CHUNK = 896
BACK_CHUNK = 896
GROUP = 128

EPSILON = 1e-06
MASKED_SCORE = -1e30
FACTOR = HEAD_DIM ** (-0.5)
VMEM_LIMIT = 50 * 1024 * 1024


def dot(first, second):
    return jnp.dot(first, second, preferred_element_type=jnp.float32)


def dot_nt(first, second):
    return lax.dot_general(
        first, second, (((1,), (1,)), ((), ())), preferred_element_type=jnp.float32
    )


def dot_tn(first, second):
    return lax.dot_general(
        first, second, (((0,), (0,)), ((), ())), preferred_element_type=jnp.float32
    )


def inverse_rms(hidden):
    return lax.rsqrt(jnp.mean(hidden * hidden, axis=-1, keepdims=True) + EPSILON)


def norm_back(hidden, inverse, gain, upstream):
    scaled = upstream * gain
    inner = jnp.mean(hidden * scaled, axis=-1, keepdims=True)
    return inverse * scaled - hidden * (inverse * inverse * inverse * inner)


def softmax_rows(scores):
    highest = jnp.max(scores, axis=-1, keepdims=True)
    weights = jnp.exp(scores - highest)
    total = jnp.sum(weights, axis=-1, keepdims=True)
    return (weights * (1.0 / total)).astype(jnp.bfloat16)


def space_forward_kernel(
    x_ref, near_ref, gain_ref, wq_ref, wk_ref, wv_ref, wo_ref,
    h_ref, q_ref, k_ref, v_ref, o_ref, p_ref,
    n_scr, bias_scr, acc_scr,
):
    step = pl.program_id(0)
    stabs = x_ref.shape[0]
    blocks, links = near_ref.shape

    @pl.when(step == 0)
    def _():
        x = x_ref[...].astype(jnp.float32)
        n_scr[...] = (x * inverse_rms(x) * gain_ref[...]).astype(jnp.bfloat16)
        acc_scr[...] = x
        lanes = lax.broadcasted_iota(jnp.int32, (blocks, blocks), 1)
        near = near_ref[...]
        listed = jnp.zeros((blocks, blocks), jnp.float32)
        for link in range(links):
            listed = jnp.where(lanes == near[:, link : link + 1], 1.0, listed)
        owner = lax.broadcasted_iota(jnp.int32, (stabs, blocks), 0) // BLOCK
        column = lax.broadcasted_iota(jnp.int32, (stabs, blocks), 1)
        widen = jnp.where(owner == column, 1.0, 0.0).astype(jnp.bfloat16)
        rows = dot(widen, listed.astype(jnp.bfloat16)).astype(jnp.bfloat16)
        bias_scr[...] = jnp.where(dot_nt(rows, widen) > 0.5, 0.0, MASKED_SCORE)

    n = n_scr[...]
    q_ref[...] = dot(n, wq_ref[...]).astype(jnp.bfloat16)
    k_ref[...] = dot(n, wk_ref[...]).astype(jnp.bfloat16)
    v_ref[...] = dot(n, wv_ref[...]).astype(jnp.bfloat16)
    for head in range(2):
        cols = slice(head * HEAD_DIM, (head + 1) * HEAD_DIM)
        keys = k_ref[:, cols]
        values = v_ref[:, cols]
        for start in range(0, stabs, CHUNK):
            rows = slice(start, start + CHUNK)
            scores = dot_nt(q_ref[rows, cols] * FACTOR, keys) + bias_scr[rows, :]
            weights = softmax_rows(scores)
            p_ref[head, rows, :] = weights
            o_ref[rows, cols] = dot(weights, values).astype(jnp.bfloat16)
    acc_scr[...] += dot(o_ref[...], wo_ref[...])

    @pl.when(step == pl.num_programs(0) - 1)
    def _():
        h_ref[...] = acc_scr[...].astype(jnp.bfloat16)


def space_backward_kernel(
    x_ref, gain_ref, g_ref, q_ref, k_ref, v_ref, o_ref, p_ref,
    wq_ref, wk_ref, wv_ref, wo_ref,
    out_ref,
    gn_scr, go_scr, gs_scr, dq_scr, dk_scr, dv_scr,
):
    step = pl.program_id(0)
    stabs = x_ref.shape[0]
    go = dot_nt(g_ref[...], wo_ref[...]).astype(jnp.bfloat16)
    go_scr[...] = go * FACTOR
    product = go.astype(jnp.float32) * o_ref[...].astype(jnp.float32)
    q_turned = q_ref[...].T
    go_turned = go.T
    for head in range(2):
        cols = slice(head * HEAD_DIM, (head + 1) * HEAD_DIM)
        keys = k_ref[:, cols]
        values = v_ref[:, cols]
        delta = jnp.sum(product[:, cols], axis=-1, keepdims=True) * FACTOR
        for start in range(0, stabs, BACK_CHUNK):
            rows = slice(start, start + BACK_CHUNK)
            grad_weights = dot_nt(go_scr[rows, cols], values)
            weights = p_ref[head, rows, :].astype(jnp.float32)
            grad_scores = (
                weights * (grad_weights - delta[start : start + BACK_CHUNK])
            ).astype(jnp.bfloat16)
            gs_scr[rows, :] = grad_scores
            dq_scr[rows, cols] = dot(grad_scores, keys).astype(jnp.bfloat16)
        dk_scr[cols, :] = dot(q_turned[cols, :], gs_scr[...]).astype(jnp.bfloat16)
        dv_scr[cols, :] = dot(go_turned[cols, :], p_ref[head]).astype(jnp.bfloat16)
    part = (
        dot_nt(dq_scr[...], wq_ref[...])
        + dot_nt(dk_scr[...].T, wk_ref[...])
        + dot_nt(dv_scr[...].T, wv_ref[...])
    )

    @pl.when(step == 0)
    def _():
        gn_scr[...] = part

    @pl.when(step > 0)
    def _():
        gn_scr[...] += part

    @pl.when(step == pl.num_programs(0) - 1)
    def _():
        x = x_ref[...].astype(jnp.float32)
        back = norm_back(x, inverse_rms(x), gain_ref[...], gn_scr[...])
        out_ref[...] = (g_ref[...].astype(jnp.float32) + back).astype(jnp.bfloat16)


def time_kernel(
    width, h_ref, side_ref, gain_ref, readout_ref, win_ref, wout_ref,
    g_ref,
    qkv_scr, p_scr, o_scr, go_scr, d_scr,
):
    total, features = h_ref.shape
    tokens = p_scr.shape[-1]
    groups = total // tokens
    hidden = h_ref[...].astype(jnp.float32)
    inverse = inverse_rms(hidden)
    gain = gain_ref[...]
    normed = (hidden * inverse * gain).astype(jnp.bfloat16)
    qkv_scr[...] = dot(normed, win_ref[...]).astype(jnp.bfloat16)
    left = lax.broadcasted_iota(jnp.int32, (tokens, tokens), 0)
    right = lax.broadcasted_iota(jnp.int32, (tokens, tokens), 1)
    kept = ((left % width) == (right % width)) & (right <= left)
    bias = jnp.where(kept, 0.0, MASKED_SCORE)
    bias = jnp.concatenate([bias, bias], axis=0)

    pairs = features // PAIR
    lanes = lax.broadcasted_iota(jnp.int32, (tokens, PAIR), 1)
    near = lanes < HEAD_DIM

    def part(index, pair):
        start = index * features + pair * PAIR
        return slice(start, start + PAIR)

    def rows_of(group):
        return pl.ds(pl.multiple_of(group * tokens, tokens), tokens)

    def stacked(block):
        empty = jnp.zeros_like(block)
        return jnp.concatenate(
            [jnp.where(near, block, empty), jnp.where(near, empty, block)], axis=0
        )

    def merged(block):
        return jnp.where(near, block[:tokens], block[tokens:]).astype(jnp.bfloat16)

    def ahead(group, carry):
        rows = rows_of(group)
        scores = [
            dot_nt(stacked(qkv_scr[rows, part(0, pair)] * FACTOR), qkv_scr[rows, part(1, pair)])
            for pair in range(pairs)
        ]
        weights = [softmax_rows(score + bias) for score in scores]
        for pair in range(pairs):
            p_scr[group * pairs + pair] = weights[pair]
        outs = [dot(weights[pair], qkv_scr[rows, part(2, pair)]) for pair in range(pairs)]
        for pair in range(pairs):
            o_scr[rows, part(0, pair)] = merged(outs[pair])
        return carry

    lax.fori_loop(0, groups, ahead, 0)
    readout = readout_ref[...]
    after = hidden + dot(o_scr[...], wout_ref[...])
    logits = jnp.sum(after * readout, axis=-1, keepdims=True)
    side = side_ref[...]
    grad_logits = (jax.nn.sigmoid(logits) - side[:, 0:1]) * side[:, 1:2]
    grad_after = grad_logits * readout
    go_scr[...] = dot_nt(grad_after.astype(jnp.bfloat16), wout_ref[...]).astype(jnp.bfloat16)

    def behind(group, carry):
        rows = rows_of(group)
        span = range(pairs)
        upstream = [stacked(go_scr[rows, part(0, pair)]) for pair in span]
        products = [dot_nt(upstream[pair], qkv_scr[rows, part(2, pair)]) for pair in span]
        weights = [p_scr[group * pairs + pair] for pair in span]
        grad_scores = []
        for pair in span:
            attended = o_scr[rows, part(0, pair)].astype(jnp.float32)
            attended = jnp.concatenate([attended, attended], axis=0)
            delta = jnp.sum(
                upstream[pair].astype(jnp.float32) * attended, axis=-1, keepdims=True
            )
            grad_scores.append(
                (weights[pair].astype(jnp.float32) * ((products[pair] - delta) * FACTOR)).astype(
                    jnp.bfloat16
                )
            )
        queries = [dot(grad_scores[pair], qkv_scr[rows, part(1, pair)]) for pair in span]
        keys = [dot_tn(grad_scores[pair], stacked(qkv_scr[rows, part(0, pair)])) for pair in span]
        values = [dot_tn(weights[pair], upstream[pair]) for pair in span]
        for pair in span:
            d_scr[rows, part(0, pair)] = merged(queries[pair])
            d_scr[rows, part(1, pair)] = keys[pair].astype(jnp.bfloat16)
            d_scr[rows, part(2, pair)] = values[pair].astype(jnp.bfloat16)
        return carry

    lax.fori_loop(0, groups, behind, 0)
    grad_normed = dot_nt(d_scr[...], win_ref[...])
    hidden = h_ref[...].astype(jnp.float32)
    back = norm_back(hidden, inverse, gain, grad_normed)
    g_ref[...] = (grad_logits * readout + back).astype(jnp.bfloat16)


def whole(*shape):
    return pl.BlockSpec(shape, lambda step: (0,) * len(shape))


def weight_specs(features):
    pairs = features // PAIR
    return [
        pl.BlockSpec((features, PAIR), lambda step: (0, step)),
        pl.BlockSpec((features, PAIR), lambda step: (0, pairs + step)),
        pl.BlockSpec((features, PAIR), lambda step: (0, 2 * pairs + step)),
        pl.BlockSpec((PAIR, features), lambda step: (step, 0)),
    ]


def space_forward(x, neighbours, gain, w_in, w_out):
    stabs, features = x.shape
    pairs = features // PAIR
    column = pl.BlockSpec((stabs, PAIR), lambda step: (0, step))
    rows = jax.ShapeDtypeStruct((stabs, features), jnp.bfloat16)
    square = pl.BlockSpec((2, stabs, stabs), lambda step: (step, 0, 0))
    return pl.pallas_call(
        space_forward_kernel,
        grid=(pairs,),
        in_specs=[whole(stabs, features), whole(*neighbours.shape), whole(1, features)]
        + weight_specs(features),
        out_specs=[whole(stabs, features), column, column, column, column, square],
        out_shape=[
            rows, rows, rows, rows, rows,
            jax.ShapeDtypeStruct((2 * pairs, stabs, stabs), jnp.bfloat16),
        ],
        scratch_shapes=[
            pltpu.VMEM((stabs, features), jnp.bfloat16),
            pltpu.VMEM((stabs, stabs), jnp.float32),
            pltpu.VMEM((stabs, features), jnp.float32),
        ],
        compiler_params=pltpu.CompilerParams(vmem_limit_bytes=VMEM_LIMIT),
        name="space_forward",
    )(x, neighbours, gain, w_in, w_in, w_in, w_out)


def space_backward(x, gain, grad, saved, w_in, w_out):
    stabs, features = x.shape
    pairs = features // PAIR
    column = pl.BlockSpec((stabs, PAIR), lambda step: (0, step))
    square = pl.BlockSpec((2, stabs, stabs), lambda step: (step, 0, 0))
    return pl.pallas_call(
        space_backward_kernel,
        grid=(pairs,),
        in_specs=[whole(stabs, features), whole(1, features), whole(stabs, features)]
        + [column] * 4
        + [square]
        + weight_specs(features),
        out_specs=whole(stabs, features),
        out_shape=jax.ShapeDtypeStruct((stabs, features), jnp.bfloat16),
        scratch_shapes=[
            pltpu.VMEM((stabs, features), jnp.float32),
            pltpu.VMEM((stabs, PAIR), jnp.bfloat16),
            pltpu.VMEM((stabs, stabs), jnp.bfloat16),
            pltpu.VMEM((stabs, PAIR), jnp.bfloat16),
            pltpu.VMEM((PAIR, stabs), jnp.bfloat16),
            pltpu.VMEM((PAIR, stabs), jnp.bfloat16),
        ],
        compiler_params=pltpu.CompilerParams(vmem_limit_bytes=VMEM_LIMIT),
        name="space_backward",
    )(x, gain, grad, *saved, w_in, w_in, w_in, w_out)


def time_both(hidden, side, gain, readout, w_in, w_out, width, tokens):
    total, features = hidden.shape
    return pl.pallas_call(
        functools.partial(time_kernel, width),
        out_shape=jax.ShapeDtypeStruct((total, features), jnp.bfloat16),
        scratch_shapes=[
            pltpu.VMEM((total, 3 * features), jnp.bfloat16),
            pltpu.VMEM((total // tokens * (features // PAIR), 2 * tokens, tokens), jnp.bfloat16),
            pltpu.VMEM((total, features), jnp.bfloat16),
            pltpu.VMEM((total, features), jnp.bfloat16),
            pltpu.VMEM((total, 3 * features), jnp.bfloat16),
        ],
        compiler_params=pltpu.CompilerParams(vmem_limit_bytes=VMEM_LIMIT),
        name="time_both",
    )(hidden, side, gain, readout, w_in, w_out)


def body(
    round_size,
    stab_size,
    inputs,
    labels,
    neighbours,
    space_in_weights,
    space_out_weights,
    space_gain,
    time_in_weights,
    time_out_weights,
    time_gain,
    readout,
):
    rounds_here, stabs_here, features = inputs.shape
    rounds = rounds_here * round_size
    stabs = stabs_here * stab_size
    copies = stab_size // rounds_here
    assert copies * rounds_here == stab_size
    padded = -(-stabs_here // round_size) * round_size
    part = padded // round_size
    direct = copies == 1 and padded == stabs_here
    both = ("round", "stab")
    space_gain, time_gain, readout = space_gain[None], time_gain[None], readout[None]

    def to_rounds(tokens):
        if copies > 1:
            tokens = jnp.repeat(tokens, copies, axis=0)
        return lax.all_to_all(tokens, "stab", split_axis=0, concat_axis=1, tiled=True)[0]

    def to_tokens(rows):
        split = rows.reshape(stab_size, stabs_here, features)
        moved = lax.all_to_all(split, "stab", split_axis=0, concat_axis=0, tiled=True)
        return moved[::copies] if copies > 1 else moved

    def pad_stabs(tokens):
        return jnp.pad(tokens, ((0, 0), (0, padded - stabs_here), (0, 0)))

    def to_times(rows):
        if direct:
            return lax.all_to_all(
                rows.reshape(rounds, part, features), both, split_axis=0, concat_axis=0, tiled=True
            )
        tokens = pad_stabs(to_tokens(rows))
        return lax.all_to_all(tokens, "round", split_axis=1, concat_axis=0, tiled=True)

    def from_times(times):
        if direct:
            moved = lax.all_to_all(times, both, split_axis=0, concat_axis=0, tiled=True)
            return moved.reshape(stabs, features)
        tokens = lax.all_to_all(times, "round", split_axis=0, concat_axis=1, tiled=True)
        return to_rounds(tokens[:, :stabs_here])

    here_round, here_stab = lax.axis_index("round"), lax.axis_index("stab")
    if direct:
        first = (here_round * stab_size + here_stab) * part
        chunks = jnp.transpose(labels.reshape(rounds_here, round_size, part), (1, 0, 2))
        sent = jnp.tile(chunks.reshape(round_size, rounds_here * part), (stab_size, 1))
        came = lax.all_to_all(sent, both, split_axis=0, concat_axis=0, tiled=True)
        came = came.reshape(round_size, stab_size, rounds_here, part)
        owner = (here_round * stab_size + here_stab) // round_size
        targets = lax.dynamic_index_in_dim(came, owner, 1, keepdims=False)
        targets = targets.reshape(rounds, part).astype(jnp.float32)
    else:
        first = here_stab * stabs_here + here_round * part
        labels_all = lax.all_gather(labels, both, axis=0, tiled=False)
        labels_all = labels_all.reshape(round_size, stab_size, rounds_here, stabs_here)
        labels_all = jnp.transpose(labels_all, (0, 2, 1, 3)).reshape(rounds, stabs)
        labels_all = jnp.pad(labels_all, ((0, 0), (0, padded)))
        targets = lax.dynamic_slice(labels_all, (0, first), (rounds, part)).astype(jnp.float32)
    slot = jnp.arange(part) + (here_round * part if not direct else 0)
    real = first + jnp.arange(part) < STABS_REAL
    if not direct:
        real = real & (slot < stabs_here)
    side = jnp.stack([targets, jnp.broadcast_to(real.astype(jnp.float32), targets.shape)], axis=-1)

    width = max(1, GROUP // rounds)
    while part % width:
        width -= 1
    groups = part // width
    tokens = width * rounds

    def to_groups(times):
        depth = times.shape[-1]
        split = times.reshape(rounds, groups, width, depth)
        return jnp.transpose(split, (1, 0, 2, 3)).reshape(groups * tokens, depth)

    def from_groups(rows):
        split = rows.reshape(groups, rounds, width, features)
        return jnp.transpose(split, (1, 0, 2, 3)).reshape(rounds, part, features)

    x = to_rounds(inputs)
    after_space, *saved = space_forward(
        x, neighbours, space_gain, space_in_weights, space_out_weights
    )
    times = to_groups(to_times(after_space))
    grad_times = time_both(
        times, to_groups(side), time_gain, readout, time_in_weights, time_out_weights, width, tokens
    )
    grad_space = from_times(from_groups(grad_times))
    grad = space_backward(x, space_gain, grad_space, saved, space_in_weights, space_out_weights)
    return to_tokens(grad).astype(jnp.float32)


def solution(mesh):
    in_specs = (
        P("round", "stab", None),
        P("round", "stab"),
        P(),
        P(),
        P(),
        P(),
        P(),
        P(),
        P(),
        P(),
    )
    out_specs = P("round", "stab", None)
    sized = functools.partial(body, mesh.shape["round"], mesh.shape["stab"])
    return jax.shard_map(sized, mesh=mesh, in_specs=in_specs, out_specs=out_specs, check_vma=False)
```
